768 devices in a mesh: group: 4 (over y_hi), dom: 48 (over z, x), sub: 4 (over y_lo, core).
Axes of the slice: x: 4, y: 8 (y_hi: 4, y_lo: 2; y = y_hi * 2 + y_lo), z: 12, core: 2. Of those that a mesh axis runs over, the one named last changes fastest.
Arguments:
- fourier: float32 [1152, 4, 128, 192], P('dom', None, ('group', 'sub')), may hold values from -6 to 6
- legendre: float32 [96, 1152, 640], P('dom'), may hold values from -0.1875 to 0.1875
- eta_start: float32 [256, 6144], P(('group', 'sub'), 'dom'), may hold values from -6 to 6
- coefs: float32 [9, 256, 6144], P(None, ('group', 'sub'), 'dom'), may hold values from 0.1 to 1
- wet: int32 [256, 6144], P(('group', 'sub'), 'dom'), may hold values 0 or 1
- src_index: int32 [256, 48, 2], P(('group', 'sub'), 'dom'), may hold values from 0 to 1727
- regrid_weight: float32 [256, 48, 2, 128, 128], P(('group', 'sub'), 'dom'), may hold values from -0.375 to 0.375
Outputs:
- spectral: float32 [96, 4, 128, 2, 640], P('dom', None, ('group', 'sub'))
- eta_final: float32 [256, 6144], P(('group', 'sub'), 'dom')
The draws below stay inside these ranges and needn't reach their ends.
All inputs are finite; a program needn't handle non-finite values. No bound on the sum of `wet` on one device may be relied on, other than what follows from the above.
Results may differ from the reference program's by a relative error of at most 0.00011.
Values sent between devices are 32-bit elements; how exact they have to be, the bound alone decides.
No kernel may reach another device: no remote copies, remote signals or barrier semaphores. Data moves between devices by JAX's collectives and lax.ppermute only.
A program may use at most 64 MiB of HBM per device.

```python
import math
import jax
import jax.numpy as jnp
from jax import lax

LAT = 1152
NDEG = 640
VARS = 4
LEV_DEV = 8
ROWS_DEV = 16
BLK = 128
KSRC = 2
SUBS = 8
M = 96
LEV = 128
BANDS = 16
SRC_ALL = 1728
OROWS = 256
OCOLS = 6144
N_DOM = 48


def touch_ends(values, stream_key, low, top_value):
    longest = values.shape.index(max(values.shape))
    spots = []
    for shift in (0, 1):
        where = [jax.random.randint(jax.random.fold_in(stream_key, axis), (), 0, length) for axis, length in enumerate(values.shape)]
        where[longest] = (where[longest] + shift) % values.shape[longest]
        spots.append(tuple(where))
    return values.at[spots[0]].set(low).at[spots[1]].set(top_value)


def shard_levels(own_key, shape, pieces, smallest, high):
    factor_of = 1.0
    for axis_at, blocks in pieces:
        heights = jax.random.uniform(jax.random.fold_in(jax.random.fold_in(own_key, 6), axis_at), (blocks,), jnp.float32, smallest / len(pieces), high / len(pieces))
        factor_of = factor_of * jnp.repeat(jnp.exp(heights), shape[axis_at] // blocks).reshape((-1,) + (1,) * (len(shape) - 1 - axis_at))
    return factor_of


def scatter_about(stream_key, extent, deviation, reach, cuts=(), kind=jnp.bfloat16):
    level = shard_levels(stream_key, extent, cuts, -0.22, 0.18) if cuts else 1.0
    result = jax.random.normal(stream_key, extent, jnp.float32) * deviation * level
    return jnp.minimum(jnp.maximum(result, -reach), reach).astype(kind)


def setup_inputs(seed: int = 0) -> dict:
    streams_of = jax.random.split(jax.random.key(seed), 8)
    fourier = scatter_about(streams_of[0], (LAT, VARS, LEV, 2 * M), 1.0, 6.0, ((0, 48), (2, 16)), jnp.float32)
    legendre = scatter_about(streams_of[1], (M, LAT, NDEG), LAT ** -0.5, 0.1875, ((0, 48),), jnp.float32)
    eta_start = scatter_about(streams_of[2], (OROWS, OCOLS), 1.0, 6.0, ((0, 16), (1, 48)), jnp.float32)
    coefs = jnp.clip(jnp.exp(math.log(1.0) - 2.3025851 * jax.random.uniform(streams_of[3], (9, OROWS, OCOLS), jnp.float32) ** shard_levels(streams_of[3], (9, OROWS, OCOLS), ((1, 16), (2, 48)), -0.2, 0.2)), 0.1, 1.0)
    wet = touch_ends((jax.random.randint(streams_of[4], (OROWS, OCOLS), 0, 8) < 7).astype(jnp.int32), jax.random.fold_in(streams_of[4], 1), 0, 1)
    src_index = touch_ends(jax.random.randint(streams_of[5], (OROWS, N_DOM, KSRC), 0, SRC_ALL), jax.random.fold_in(streams_of[5], 1), 0, SRC_ALL - 1).astype(jnp.int32)
    regrid_weight = scatter_about(streams_of[6], (OROWS, N_DOM, KSRC, BLK, BLK), (BLK * KSRC) ** -0.5, 0.375, ((0, 16), (1, 48)), jnp.float32)
    return dict(fourier=fourier, legendre=legendre, eta_start=eta_start, coefs=coefs, wet=wet, src_index=src_index, regrid_weight=regrid_weight)


forcing_rate = 0.5


def reference(fourier, legendre, eta_start, coefs, wet, src_index, regrid_weight):
    parts = fourier.reshape(LAT, VARS, LEV, M, 2)
    spectral = jnp.einsum('man,avlmr->mvlrn', legendre, parts, precision=lax.Precision.HIGHEST)
    surface = fourier[:, 0, ::LEV_DEV, :]
    flux = jnp.transpose(surface, (1, 0, 2)).reshape(BANDS, SRC_ALL, BLK)
    band = (jnp.arange(OROWS) // ROWS_DEV).astype(jnp.int32)
    picked = flux[band[:, None, None], src_index]
    forcing = jnp.einsum('rdkts,rdks->rdt', regrid_weight, picked, precision=lax.Precision.HIGHEST)
    forcing = forcing.reshape(OROWS, OCOLS)
    norm = coefs / jnp.sum(coefs, axis=0)
    wetness = wet.astype(jnp.float32)
    eta = eta_start
    for cycle in range(SUBS):
        padded = jnp.pad(eta, 1)
        total = norm[0] * padded[0:OROWS, 0:OCOLS]
        for index in range(1, 9):
            shift_row = index // 3
            shift_col = index % 3
            total = total + norm[index] * padded[shift_row:shift_row + OROWS, shift_col:shift_col + OCOLS]
        eta = wetness * (total + forcing_rate * forcing)
    return spectral, eta
```

```python
import jax
import jax.numpy as jnp
from jax import lax
from jax.experimental import pallas as pl
from jax.experimental.pallas import tpu as pltpu
from jax.sharding import Mesh
from jax.sharding import PartitionSpec as P

SUBS = 8
DOM = ("dom_0", "dom_1")
ROW = ("group", "sub")
FORCING_RATE = 0.5
FIELDS = 11
PIECE = 40
EDGE = 8


def flux_kernel(x_ref, out_ref):
    copies = out_ref.shape[0]
    rows = []
    for pair in range(x_ref.shape[0] // 2):
        a = x_ref[2 * pair, 0:1, :]
        b = x_ref[2 * pair + 1, 0:1, :]
        rows.append(a[:, :128])
        rows.append(jnp.concatenate([a[:, 128:], b[:, :64]], axis=1))
        rows.append(b[:, 64:])
    rows.append(jnp.zeros((PIECE - len(rows), 128), jnp.float32))
    piece = jnp.concatenate(rows, axis=0)
    for copy in range(copies):
        out_ref[copy] = piece


def flux_pieces(fourier, copies):
    lat, _, lev, cols = fourier.shape
    return pl.pallas_call(
        flux_kernel,
        out_shape=jax.ShapeDtypeStruct((copies, PIECE, 128), jnp.float32),
        grid=(1,),
        in_specs=[pl.BlockSpec((lat, None, lev, cols), lambda i: (0, 0, 0, 0))],
        out_specs=pl.BlockSpec((copies, PIECE, 128), lambda i: (0, 0, 0)),
        name="flux_pieces",
    )(fourier)


def pack_kernel(x_ref, out_ref):
    sub = lax.broadcasted_iota(jnp.int32, (24, 8, 128), 1)
    lane = lax.broadcasted_iota(jnp.int32, (24, 8, 128), 2) // 32
    halves = []
    for half in range(2):
        x = x_ref[pl.ds(half * 128, 128), :]
        t = jnp.concatenate(
            [jnp.transpose(x[:, :128]), jnp.transpose(x[:, 128:])], axis=0
        )
        t = t.reshape(24, 8, 128)
        for bit in (1, 2):
            up = pltpu.roll(pltpu.roll(t, 8 - bit, axis=1), 32 * bit, axis=2)
            down = pltpu.roll(pltpu.roll(t, bit, axis=1), 128 - 32 * bit, axis=2)
            row_bit = (sub & bit) != 0
            lane_bit = (lane & bit) != 0
            t = jnp.where(
                row_bit == lane_bit, t, jnp.where(lane_bit, up, down)
            )
        halves.append(t)
    first, second = halves
    low = sub < 4
    out_ref[:, 0] = jnp.where(low, first, pltpu.roll(second, 4, axis=1))
    out_ref[:, 1] = jnp.where(low, pltpu.roll(first, 4, axis=1), second)


def pack(fourier):
    lat = fourier.shape[0]
    rows = fourier.shape[1] * fourier.shape[2]
    flat = fourier.reshape(lat * rows, fourier.shape[3])
    out = pl.pallas_call(
        pack_kernel,
        out_shape=jax.ShapeDtypeStruct((24, 2, lat, 128), jnp.float32),
        grid=(lat // 8,),
        in_specs=[pl.BlockSpec((8 * rows, flat.shape[1]), lambda i: (i, 0))],
        out_specs=pl.BlockSpec((24, 2, 8, 128), lambda i: (0, 0, i, 0)),
        name="pack",
    )(flat)
    return out.reshape(48, lat, 128)


def edges_kernel(coefs_ref, wet_ref, eta_ref, index_ref, w_low_ref, w_high_ref, fields_ref, low_ref, high_ref):
    coefs = coefs_ref[...]
    norm = coefs / jnp.sum(coefs, axis=0)
    fields_ref[0:9] = norm
    fields_ref[9] = wet_ref[...].astype(jnp.float32)
    fields_ref[10] = eta_ref[...]
    first = jnp.transpose(fields_ref[0:8].reshape(128, 128))
    second = jnp.transpose(
        jnp.concatenate(
            [fields_ref[8:11].reshape(48, 128), jnp.zeros((80, 128), jnp.float32)], axis=0
        )
    )
    index = index_ref[...].astype(jnp.float32)
    for ref, w_ref, at in ((low_ref, w_low_ref, 0), (high_ref, w_high_ref, 120)):
        ref[0:256] = w_ref[...].reshape(256, 128)
        ref[256:264] = first[at : at + 8]
        ref[264:272] = second[at : at + 8]
        ref[272:280] = jnp.zeros((8, 128), jnp.float32)
        ref[272:274, 0:16] = index


def edges(coefs, wet, eta, index, weight):
    rows = eta.shape[0]
    message = jax.ShapeDtypeStruct((280, 128), jnp.float32)
    whole = lambda shape: pl.BlockSpec(shape, lambda i: (0,) * len(shape))
    return pl.pallas_call(
        edges_kernel,
        out_shape=(jax.ShapeDtypeStruct((FIELDS, rows, 128), jnp.float32), message, message),
        grid=(1,),
        in_specs=[
            whole(coefs.shape),
            whole(wet.shape),
            whole(eta.shape),
            whole(index.shape),
            pl.BlockSpec((32, 8, 128), lambda i: (0, 0, 0)),
            pl.BlockSpec((32, 8, 128), lambda i: (0, 15, 0)),
        ],
        out_specs=(whole((FIELDS, rows, 128)), whole((280, 128)), whole((280, 128))),
        name="edges",
    )(coefs, wet, eta, index, weight, weight)


def forcing_kernel(own_ref, right_ref, left_ref, flux_ref, w_ref, fields_ref, from_right_ref, from_left_ref, top_ref, low_ref, picks):
    for place, ref in enumerate((own_ref, right_ref, left_ref)):
        for i in range(16):
            for k in range(2):
                picks[place, pl.ds(2 * i + k, 1), :] = flux_ref[pl.ds(ref[k, i], 1), :]
    sub = lax.broadcasted_iota(jnp.int32, (16, 8, 128), 1)
    tile = lax.broadcasted_iota(jnp.int32, (16, 8, 128), 0)
    lane = lax.broadcasted_iota(jnp.int32, (16, 8, 128), 2)
    here = lane == 8 * tile + sub
    for i in range(16):
        acc = w_ref[2 * i] * picks[0, pl.ds(2 * i, 1), :]
        acc = acc + w_ref[2 * i + 1] * picks[0, pl.ds(2 * i + 1, 1), :]
        total = jnp.sum(acc.reshape(16, 8, 128), axis=2, keepdims=True)
        row = jnp.sum(jnp.sum(jnp.where(here, total, 0.0), axis=0), axis=0, keepdims=True)
        ref = top_ref if i < 8 else low_ref
        ref[FIELDS, 0, pl.ds(i % 8, 1), :] = row
    wide_r = (from_right_ref[0:256] * jnp.broadcast_to(picks[1][:, None, :], (32, 8, 128)).reshape(256, 128)).reshape(16, 2, 8, 128)
    wide_l = (from_left_ref[0:256] * jnp.broadcast_to(picks[2][:, None, :], (32, 8, 128)).reshape(256, 128)).reshape(16, 2, 8, 128)
    sum_r = jnp.sum(wide_r[:, 0] + wide_r[:, 1], axis=2, keepdims=True)
    sum_l = jnp.sum(wide_l[:, 0] + wide_l[:, 1], axis=2, keepdims=True)
    outer = jnp.where(lane == sub, sum_r, jnp.where(lane == 120 + sub, sum_l, 0.0))
    outer = jnp.sum(outer, axis=1)
    top_ref[FIELDS, 1] = outer[0:8]
    low_ref[FIELDS, 1] = outer[8:16]
    gap = jnp.zeros((112, 128), jnp.float32)
    side = [
        jnp.transpose(
            jnp.concatenate([from_right_ref[at : at + 8], gap, from_left_ref[at : at + 8]], axis=0)
        ).reshape(8, 16, 128)
        for at in (256, 264)
    ]
    for f in range(FIELDS):
        centre = fields_ref[f]
        beside = side[f // 8][f % 8]
        top_ref[f, 0] = centre[0:8]
        low_ref[f, 0] = centre[8:16]
        top_ref[f, 1] = beside[0:8]
        low_ref[f, 1] = beside[8:16]


def forcing_fields(own, right, left, flux, weight, fields, from_right, from_left):
    half = jax.ShapeDtypeStruct((FIELDS + 1, 2, 8, 128), jnp.float32)
    smem = pl.BlockSpec(memory_space=pltpu.SMEM)
    vmem = pl.BlockSpec(memory_space=pltpu.VMEM)
    return pl.pallas_call(
        forcing_kernel,
        out_shape=(half, half),
        in_specs=[smem] * 3 + [vmem] * 5,
        out_specs=(vmem, vmem),
        scratch_shapes=[pltpu.VMEM((3, 32, 128), jnp.float32)],
        name="forcing",
    )(own, right, left, flux, weight, fields, from_right, from_left)


def relax_kernel(top_ref, low_ref, below_ref, above_ref, out_ref, table):
    for f in range(FIELDS + 1):
        for place, ref in enumerate((top_ref, low_ref, below_ref, above_ref)):
            for side in range(2):
                table[f, place * 8 : place * 8 + 8, side * 128 : side * 128 + 128] = ref[f, side]
    norm = []
    for k in range(9):
        value = table[k]
        if k // 3 == 0:
            value = pltpu.roll(value, 31, axis=0)
        if k // 3 == 2:
            value = pltpu.roll(value, 1, axis=0)
        norm.append(value)
    wet = table[9]
    eta = table[10]
    force = FORCING_RATE * table[11]
    for _ in range(SUBS):
        left = pltpu.roll(eta, 1, axis=1)
        right = pltpu.roll(eta, 255, axis=1)
        part = [norm[3 * p] * left + norm[3 * p + 1] * eta + norm[3 * p + 2] * right for p in range(3)]
        total = pltpu.roll(part[0], 1, axis=0) + part[1] + pltpu.roll(part[2], 31, axis=0)
        eta = wet * (total + force)
    out_ref[...] = eta[0:16, 0:128]


def relax(top, low, below, above):
    vmem = pl.BlockSpec(memory_space=pltpu.VMEM)
    return pl.pallas_call(
        relax_kernel,
        out_shape=jax.ShapeDtypeStruct((16, 128), jnp.float32),
        in_specs=[vmem] * 4,
        out_specs=vmem,
        scratch_shapes=[pltpu.VMEM((FIELDS + 1, 32, 256), jnp.float32)],
        name="relax",
    )(top, low, below, above)


def split(value):
    high = value.astype(jnp.bfloat16)
    return high, (value - high.astype(jnp.float32)).astype(jnp.bfloat16)


def contract_kernel(x_ref, leg_ref, out_ref, acc):
    m, step = pl.program_id(0), pl.program_id(1)
    depth = leg_ref.shape[1]
    x = jnp.transpose(x_ref[...])
    x = jnp.where(m == 0, x[0:64], x[64:128])
    x_high, x_low = split(x)
    high, low = split(leg_ref[0])
    dot = lambda a, b: jnp.dot(a, b, preferred_element_type=jnp.float32)
    both = dot(jnp.concatenate([x_high, x_low], axis=0), high)
    part = both[0:64] + both[64:128] + dot(x_high, low)

    @pl.when(step == 0)
    def _():
        acc[...] = part

    @pl.when(step > 0)
    def _():
        acc[...] = acc[...] + part

    @pl.when(step == pl.num_programs(1) - 1)
    def _():
        for r in range(2):
            for c in range(5):
                out_ref[0, pl.ds(2 * c + r, 32, stride=10), :] = acc[
                    r * 32 : r * 32 + 32, c * 128 : c * 128 + 128
                ]


def contract(x, legendre):
    ms, depth, degrees = legendre.shape
    chunk = depth // 3
    out = pl.pallas_call(
        contract_kernel,
        out_shape=jax.ShapeDtypeStruct((ms, 320, 128), jnp.float32),
        grid=(ms, 3),
        in_specs=[
            pl.BlockSpec((chunk, 128), lambda m, k: (k, 0)),
            pl.BlockSpec((1, chunk, degrees), lambda m, k: (m, k, 0)),
        ],
        out_specs=pl.BlockSpec((1, 320, 128), lambda m, k: (m, 0, 0)),
        scratch_shapes=[pltpu.VMEM((64, degrees), jnp.float32)],
        name="contract",
    )(x, legendre)
    out = out.reshape(ms, 32, 5, 2, 128).transpose(0, 1, 3, 2, 4)
    return out.reshape(ms, 4, 8, 2, degrees)


def shifted(value, axis, step):
    count = lax.axis_size(axis)
    pairs = [(i, i + step) for i in range(count) if 0 <= i + step < count]
    return lax.ppermute(value, axis, pairs)


def place_of(index):
    device, within = index // 36, index % 36
    return ((device % 4) * 12 + device // 4) * PIECE + within


def body(fourier, legendre, eta_start, coefs, wet, src_index, regrid_weight):
    weight = regrid_weight.reshape(32, 128, 128)
    index = jnp.transpose(src_index[:, 0, :])
    pieces = flux_pieces(fourier, 12)
    along = lax.all_to_all(pieces, "dom_0", split_axis=0, concat_axis=0)
    packed = pack(fourier)
    fields, low_edge, high_edge = edges(coefs, wet, eta_start, index, weight)
    from_right = shifted(low_edge, DOM, -1)
    from_left = shifted(high_edge, DOM, 1)
    spread = jnp.broadcast_to(along.reshape(1, 12 * PIECE, 128), (4, 12 * PIECE, 128))
    packed, spread = lax.optimization_barrier((packed, spread))
    flux = lax.all_to_all(spread, "dom_1", split_axis=0, concat_axis=0)
    block = lax.all_to_all(packed, DOM, split_axis=0, concat_axis=0)
    own = place_of(index)
    right = place_of(from_right[272:274, 0:16].astype(jnp.int32))
    left = place_of(from_left[272:274, 0:16].astype(jnp.int32))
    top, low = forcing_fields(
        own, right, left, flux.reshape(48 * PIECE, 128), weight, fields, from_right, from_left
    )
    below = shifted(top, ROW, -1)
    above = shifted(low, ROW, 1)
    eta = relax(top, low, below, above)
    spectral = contract(block.reshape(1152, 128), legendre)
    return spectral, eta


def solution(mesh):
    torus = Mesh(
        mesh.devices.reshape(mesh.shape["group"], 12, 4, mesh.shape["sub"]),
        ("group", "dom_0", "dom_1", "sub"),
    )
    in_specs = (
        P(DOM, None, ROW, None),
        P(DOM, None, None),
        P(ROW, DOM),
        P(None, ROW, DOM),
        P(ROW, DOM),
        P(ROW, DOM, None),
        P(ROW, DOM, None, None, None),
    )
    out_specs = (P(DOM, None, ROW, None, None), P(ROW, DOM))
    return jax.shard_map(body, mesh=torus, in_specs=in_specs, out_specs=out_specs, check_vma=False)
```

```python
import jax
import jax.numpy as jnp
from jax import lax
from jax.experimental import pallas as pl
from jax.experimental.pallas import tpu as pltpu
from jax.sharding import Mesh
from jax.sharding import PartitionSpec as P


SUBS = 8
DOM = ("dom_0", "dom_1")
ROW = ("group", "sub")
FORCING_RATE = 0.5
FIELDS = 11
PIECE = 40


VMEM = pl.BlockSpec(memory_space=pltpu.VMEM)
SMALL = pltpu.CompilerParams(vmem_limit_bytes=24 << 20)


def in_vmem(value):
    return pltpu.with_memory_space_constraint(value, pltpu.VMEM)


def in_hbm(value):
    return pltpu.with_memory_space_constraint(value, pltpu.HBM)


def flux_kernel(x_ref, out_ref):
    copies = out_ref.shape[0]
    rows = []
    for pair in range(x_ref.shape[0] // 2):
        a = x_ref[2 * pair, 0:1, :]
        b = x_ref[2 * pair + 1, 0:1, :]
        rows.append(a[:, :128])
        rows.append(jnp.concatenate([a[:, 128:], b[:, :64]], axis=1))
        rows.append(b[:, 64:])
    rows.append(jnp.zeros((PIECE - len(rows), 128), jnp.float32))
    piece = jnp.concatenate(rows, axis=0)
    for copy in range(copies):
        out_ref[copy] = piece


def flux_pieces(fourier, copies):
    lat, _, lev, cols = fourier.shape
    return pl.pallas_call(
        flux_kernel,
        out_shape=jax.ShapeDtypeStruct((copies, PIECE, 128), jnp.float32),
        grid=(1,),
        in_specs=[pl.BlockSpec((lat, None, lev, cols), lambda i: (0, 0, 0, 0))],
        out_specs=pl.BlockSpec((copies, PIECE, 128), lambda i: (0, 0, 0)),
        compiler_params=SMALL,
        name="flux_pieces",
    )(in_hbm(fourier))


def pack_kernel(x_ref, out_ref):
    turn = lax.broadcasted_iota(jnp.int32, (32, 128), 1) % 4
    tiles = []
    for part in range(3):
        lats = []
        for j in range(4):
            if part < 2:
                lats.append(x_ref[pl.ds((4 * part + j) * 32, 32), 0:128])
            else:
                ends = [x_ref[pl.ds((4 * half + j) * 32, 32), 128:192] for half in range(2)]
                lats.append(jnp.concatenate(ends, axis=1))
        groups = []
        for c in range(4):
            moved = [x if j == c else pltpu.roll(x, (j - c) % 128, axis=1) for j, x in enumerate(lats)]
            low = jnp.where(turn == 0, moved[0], moved[1])
            high = jnp.where(turn == 2, moved[2], moved[3])
            groups.append(jnp.where(turn < 2, low, high))
        tiles.append(jnp.transpose(jnp.concatenate(groups, axis=0)))
    first = jnp.concatenate([tiles[0], tiles[2][0:64]], axis=0).reshape(24, 8, 128)
    second = jnp.concatenate([tiles[1], tiles[2][64:128]], axis=0).reshape(24, 8, 128)
    upper = lax.broadcasted_iota(jnp.int32, (24, 8, 128), 1) < 4
    out_ref[:, 0] = jnp.where(upper, first, pltpu.roll(second, 4, axis=1))
    out_ref[:, 1] = jnp.where(upper, pltpu.roll(first, 4, axis=1), second)


def pack(fourier):
    lat = fourier.shape[0]
    rows = fourier.shape[1] * fourier.shape[2]
    flat = fourier.reshape(lat * rows, fourier.shape[3])
    out = pl.pallas_call(
        pack_kernel,
        out_shape=pltpu.HBM((24, 2, lat, 128), jnp.float32),
        grid=(lat // 8,),
        in_specs=[pl.BlockSpec((8 * rows, flat.shape[1]), lambda i: (i, 0))],
        out_specs=pl.BlockSpec((24, 2, 8, 128), lambda i: (0, 0, i, 0)),
        compiler_params=SMALL,
        name="pack",
    )(in_hbm(flat))
    return out.reshape(48, lat, 128)


def edges_kernel(coefs_ref, wet_ref, eta_ref, index_ref, w_low_ref, w_high_ref, fields_ref, places_ref, low_ref, high_ref):
    coefs = coefs_ref[...]
    norm = coefs / jnp.sum(coefs, axis=0)
    fields_ref[0:9] = norm
    fields_ref[9] = wet_ref[...].astype(jnp.float32)
    fields_ref[10] = eta_ref[...]
    first = jnp.transpose(fields_ref[0:8].reshape(128, 128))
    second = jnp.transpose(
        jnp.concatenate(
            [fields_ref[8:11].reshape(48, 128), jnp.zeros((80, 128), jnp.float32)], axis=0
        )
    )
    index = index_ref[...]
    device = (index * 1821) >> 16
    places = ((device & 3) * 12 + (device >> 2)) * PIECE + index - device * 36
    places_ref[...] = places
    for ref, w_ref, at in ((low_ref, w_low_ref, 0), (high_ref, w_high_ref, 120)):
        ref[0:256] = w_ref[...].reshape(256, 128)
        ref[256:264] = first[at : at + 8]
        ref[264:272] = second[at : at + 8]
        ref[272:280] = jnp.zeros((8, 128), jnp.float32)
        ref[272:274, 0:16] = places.astype(jnp.float32)


def edges(coefs, wet, eta, index, weight):
    rows = eta.shape[0]
    message = jax.ShapeDtypeStruct((280, 128), jnp.float32)
    whole = lambda shape: pl.BlockSpec(shape, lambda i: (0,) * len(shape))
    return pl.pallas_call(
        edges_kernel,
        out_shape=(
            jax.ShapeDtypeStruct((FIELDS, rows, 128), jnp.float32),
            jax.ShapeDtypeStruct(index.shape, jnp.int32),
            message,
            message,
        ),
        grid=(1,),
        in_specs=[
            whole(coefs.shape),
            whole(wet.shape),
            whole(eta.shape),
            whole(index.shape),
            pl.BlockSpec((32, 8, 128), lambda i: (0, 0, 0)),
            pl.BlockSpec((32, 8, 128), lambda i: (0, 15, 0)),
        ],
        out_specs=(whole((FIELDS, rows, 128)), whole(index.shape), whole((280, 128)), whole((280, 128))),
        compiler_params=SMALL,
        name="edges",
    )(in_hbm(coefs), in_hbm(wet), in_hbm(eta), in_hbm(index), in_hbm(weight), in_hbm(weight))


def forcing_kernel(own_ref, right_ref, left_ref, flux_ref, w_ref, fields_ref, from_right_ref, from_left_ref, top_ref, low_ref, picks):
    for place, ref in enumerate((own_ref, right_ref, left_ref)):
        for i in range(16):
            for k in range(2):
                picks[place, pl.ds(2 * i + k, 1), :] = flux_ref[pl.ds(ref[k, i].astype(jnp.int32), 1), :]
    sub = lax.broadcasted_iota(jnp.int32, (16, 8, 128), 1)
    tile = lax.broadcasted_iota(jnp.int32, (16, 8, 128), 0)
    lane = lax.broadcasted_iota(jnp.int32, (16, 8, 128), 2)
    here = lane == 8 * tile + sub
    for i in range(16):
        acc = w_ref[2 * i] * picks[0, pl.ds(2 * i, 1), :]
        acc = acc + w_ref[2 * i + 1] * picks[0, pl.ds(2 * i + 1, 1), :]
        total = jnp.sum(acc.reshape(16, 8, 128), axis=2, keepdims=True)
        row = jnp.sum(jnp.sum(jnp.where(here, total, 0.0), axis=0), axis=0, keepdims=True)
        ref = top_ref if i < 8 else low_ref
        ref[FIELDS, 0, pl.ds(i % 8, 1), :] = row
    wide_r = (from_right_ref[0:256] * jnp.broadcast_to(picks[1][:, None, :], (32, 8, 128)).reshape(256, 128)).reshape(16, 2, 8, 128)
    wide_l = (from_left_ref[0:256] * jnp.broadcast_to(picks[2][:, None, :], (32, 8, 128)).reshape(256, 128)).reshape(16, 2, 8, 128)
    sum_r = jnp.sum(wide_r[:, 0] + wide_r[:, 1], axis=2, keepdims=True)
    sum_l = jnp.sum(wide_l[:, 0] + wide_l[:, 1], axis=2, keepdims=True)
    outer = jnp.where(lane == sub, sum_r, jnp.where(lane == 120 + sub, sum_l, 0.0))
    outer = jnp.sum(outer, axis=1)
    top_ref[FIELDS, 1] = outer[0:8]
    low_ref[FIELDS, 1] = outer[8:16]
    gap = jnp.zeros((112, 128), jnp.float32)
    side = [
        jnp.transpose(
            jnp.concatenate([from_right_ref[at : at + 8], gap, from_left_ref[at : at + 8]], axis=0)
        ).reshape(8, 16, 128)
        for at in (256, 264)
    ]
    for f in range(FIELDS):
        centre = fields_ref[f]
        beside = side[f // 8][f % 8]
        top_ref[f, 0] = centre[0:8]
        low_ref[f, 0] = centre[8:16]
        top_ref[f, 1] = beside[0:8]
        low_ref[f, 1] = beside[8:16]


def forcing_fields(places, flux, weight, fields, from_right, from_left):
    half = jax.ShapeDtypeStruct((FIELDS + 1, 2, 8, 128), jnp.float32)
    smem = pl.BlockSpec(memory_space=pltpu.SMEM)
    tail = pl.BlockSpec((8, 128), lambda i: (34, 0), memory_space=pltpu.SMEM)
    return pl.pallas_call(
        forcing_kernel,
        out_shape=(half, half),
        grid=(1,),
        in_specs=[smem, tail, tail] + [VMEM] * 5,
        out_specs=(VMEM, VMEM),
        scratch_shapes=[pltpu.VMEM((3, 32, 128), jnp.float32)],
        compiler_params=SMALL,
        name="forcing",
    )(places, from_right, from_left, flux, weight, fields, from_right, from_left)


def relax_kernel(top_ref, low_ref, below_ref, above_ref, leg_ref, out_ref, stage_ref, table, sem):
    copy = pltpu.make_async_copy(leg_ref.at[0], stage_ref, sem)
    copy.start()
    for f in range(FIELDS + 1):
        for place, ref in enumerate((top_ref, low_ref, below_ref, above_ref)):
            for side in range(2):
                table[f, place * 8 : place * 8 + 8, side * 128 : side * 128 + 128] = ref[f, side]
    norm = []
    for k in range(9):
        value = table[k]
        if k // 3 == 0:
            value = pltpu.roll(value, 31, axis=0)
        if k // 3 == 2:
            value = pltpu.roll(value, 1, axis=0)
        norm.append(value)
    wet = table[9]
    eta = table[10]
    force = FORCING_RATE * table[11]
    for _ in range(SUBS):
        left = pltpu.roll(eta, 1, axis=1)
        right = pltpu.roll(eta, 255, axis=1)
        part = [norm[3 * p] * left + norm[3 * p + 1] * eta + norm[3 * p + 2] * right for p in range(3)]
        total = pltpu.roll(part[0], 1, axis=0) + part[1] + pltpu.roll(part[2], 31, axis=0)
        eta = wet * (total + force)
    out_ref[...] = eta[0:16, 0:128]
    copy.wait()


def relax(top, low, below, above, legendre):
    return pl.pallas_call(
        relax_kernel,
        out_shape=(
            jax.ShapeDtypeStruct((16, 128), jnp.float32),
            pltpu.VMEM(legendre.shape[1:], jnp.float32),
        ),
        in_specs=[VMEM] * 4 + [pl.BlockSpec(memory_space=pl.ANY)],
        out_specs=(VMEM, VMEM),
        scratch_shapes=[
            pltpu.VMEM((FIELDS + 1, 32, 256), jnp.float32),
            pltpu.SemaphoreType.DMA(()),
        ],
        compiler_params=SMALL,
        name="relax",
    )(top, low, below, above, in_hbm(legendre))


def split(value):
    high = value.astype(jnp.bfloat16)
    return high, (value - high.astype(jnp.float32)).astype(jnp.bfloat16)


def contract_kernel(x_ref, first_ref, leg_ref, out_ref, second_ref, sem):
    copy = pltpu.make_async_copy(leg_ref.at[1], second_ref, sem)
    copy.start()
    x_high, x_low = split(jnp.transpose(x_ref[...]))
    dot = lambda a, b: jnp.dot(a, b, preferred_element_type=jnp.float32)
    for m, part_ref in enumerate((first_ref, second_ref)):
        if m == 1:
            copy.wait()
        mine = slice(m * 64, m * 64 + 64)
        high, low = split(part_ref[...])
        both = dot(jnp.concatenate([x_high[mine], x_low[mine]], axis=0), high)
        total = both[0:64] + both[64:128] + dot(x_high[mine], low)
        for r in range(2):
            for v in range(4):
                for l in range(8):
                    row = r * 32 + v * 8 + l
                    out_ref[m, v, l, pl.ds(r, 1), :] = total[row : row + 1]


def contract(x, first, legendre):
    degrees = first.shape[1]
    return pl.pallas_call(
        contract_kernel,
        out_shape=jax.ShapeDtypeStruct((2, 4, 8, 2, degrees), jnp.float32),
        in_specs=[VMEM, VMEM, pl.BlockSpec(memory_space=pl.ANY)],
        out_specs=VMEM,
        scratch_shapes=[pltpu.VMEM(first.shape, jnp.float32), pltpu.SemaphoreType.DMA(())],
        compiler_params=SMALL,
        name="contract",
    )(x, in_vmem(first), in_hbm(legendre))


def shifted(value, axis, step):
    count = lax.axis_size(axis)
    pairs = [(i, i + step) for i in range(count) if 0 <= i + step < count]
    return lax.ppermute(value, axis, pairs)


def body(fourier, legendre, eta_start, coefs, wet, src_index, regrid_weight):
    weight = regrid_weight.reshape(32, 128, 128)
    index = jnp.transpose(src_index[:, 0, :])
    pieces = flux_pieces(fourier, 12)
    along = lax.all_to_all(pieces, "dom_0", split_axis=0, concat_axis=0)
    packed = pack(fourier)
    fields, places, low_edge, high_edge = edges(coefs, wet, eta_start, index, weight)
    from_right = shifted(low_edge, DOM, -1)
    from_left = shifted(high_edge, DOM, 1)
    packed, along, from_right, from_left = lax.optimization_barrier((packed, along, from_right, from_left))
    block = lax.all_to_all(packed, DOM, split_axis=0, concat_axis=0)
    flux = lax.all_gather(along.reshape(12 * PIECE, 128), "dom_1", axis=0, tiled=True)
    top, low = forcing_fields(places, flux, weight, fields, from_right, from_left)
    below = shifted(top, ROW, -1)
    above = shifted(low, ROW, 1)
    eta, first = relax(top, low, below, above, legendre)
    spectral = contract(block.reshape(1152, 128), first, legendre)
    return spectral, eta


def solution(mesh):
    torus = Mesh(
        mesh.devices.reshape(mesh.shape["group"], 12, 4, mesh.shape["sub"]),
        ("group", "dom_0", "dom_1", "sub"),
    )
    in_specs = (
        P(DOM, None, ROW, None),
        P(DOM, None, None),
        P(ROW, DOM),
        P(None, ROW, DOM),
        P(ROW, DOM),
        P(ROW, DOM, None),
        P(ROW, DOM, None, None, None),
    )
    out_specs = (P(DOM, None, ROW, None, None), P(ROW, DOM))

    def step(*args):
        return body(*args)

    step = jax.shard_map(step, mesh=torus, in_specs=in_specs, out_specs=out_specs, check_vma=False)
    return step
```

```python
import jax
import jax.numpy as jnp
from jax import lax
from jax.experimental import pallas as pl
from jax.experimental.pallas import tpu as pltpu
from jax.sharding import Mesh
from jax.sharding import PartitionSpec as P


SUBS = 8
DOM = ("dom_0", "dom_1")
ROW = ("group", "sub")
FORCING_RATE = 0.5
FIELDS = 11
PIECE = 40


VMEM = pl.BlockSpec(memory_space=pltpu.VMEM)
ANY = pl.BlockSpec(memory_space=pl.ANY)
STAGED = 768
SMALL = pltpu.CompilerParams(vmem_limit_bytes=24 << 20)


def in_vmem(value):
    return pltpu.with_memory_space_constraint(value, pltpu.VMEM)


def in_hbm(value):
    return pltpu.with_memory_space_constraint(value, pltpu.HBM)


def flux_kernel(x_ref, out_ref):
    copies = out_ref.shape[0]
    rows = []
    for pair in range(x_ref.shape[0] // 2):
        a = x_ref[2 * pair, 0:1, :]
        b = x_ref[2 * pair + 1, 0:1, :]
        rows.append(a[:, :128])
        rows.append(jnp.concatenate([a[:, 128:], b[:, :64]], axis=1))
        rows.append(b[:, 64:])
    rows.append(jnp.zeros((PIECE - len(rows), 128), jnp.float32))
    piece = jnp.concatenate(rows, axis=0)
    for copy in range(copies):
        out_ref[copy] = piece


def flux_pieces(fourier, copies):
    lat, _, lev, cols = fourier.shape
    return pl.pallas_call(
        flux_kernel,
        out_shape=pltpu.VMEM((copies, PIECE, 128), jnp.float32),
        grid=(1,),
        in_specs=[pl.BlockSpec((lat, None, lev, cols), lambda i: (0, 0, 0, 0))],
        out_specs=VMEM,
        compiler_params=SMALL,
        name="flux_pieces",
    )(in_hbm(fourier))


def pack_kernel(all_ref, packed_ref, inside, outside, in_sem, out_sem):
    chunk = inside.shape[1]
    steps = inside.shape[0]
    reads = [
        pltpu.make_async_copy(all_ref.at[pl.ds(i * chunk, chunk)], inside.at[i], in_sem.at[i])
        for i in range(steps)
    ]
    writes = [
        pltpu.make_async_copy(outside.at[i], packed_ref.at[:, :, pl.ds(8 * i, 8)], out_sem.at[i])
        for i in range(steps)
    ]
    for read in reads:
        read.start()
    for read, write, x_ref, out_ref in zip(reads, writes, map(inside.at.__getitem__, range(steps)), map(outside.at.__getitem__, range(steps))):
        read.wait()
        pack_latitudes(x_ref, out_ref)
        write.start()
    for write in writes:
        write.wait()


def pack_latitudes(x_ref, out_ref):
    turn = lax.broadcasted_iota(jnp.int32, (32, 128), 1) % 4
    tiles = []
    for part in range(3):
        lats = []
        for j in range(4):
            if part < 2:
                lats.append(x_ref[pl.ds((4 * part + j) * 32, 32), 0:128])
            else:
                ends = [x_ref[pl.ds((4 * half + j) * 32, 32), 128:192] for half in range(2)]
                lats.append(jnp.concatenate(ends, axis=1))
        groups = []
        for c in range(4):
            moved = [x if j == c else pltpu.roll(x, (j - c) % 128, axis=1) for j, x in enumerate(lats)]
            low = jnp.where(turn == 0, moved[0], moved[1])
            high = jnp.where(turn == 2, moved[2], moved[3])
            groups.append(jnp.where(turn < 2, low, high))
        tiles.append(jnp.transpose(jnp.concatenate(groups, axis=0)))
    first = jnp.concatenate([tiles[0], tiles[2][0:64]], axis=0).reshape(24, 8, 128)
    second = jnp.concatenate([tiles[1], tiles[2][64:128]], axis=0).reshape(24, 8, 128)
    upper = lax.broadcasted_iota(jnp.int32, (24, 8, 128), 1) < 4
    out_ref[:, 0] = jnp.where(upper, first, pltpu.roll(second, 4, axis=1))
    out_ref[:, 1] = jnp.where(upper, pltpu.roll(first, 4, axis=1), second)


def pack(fourier):
    lat = fourier.shape[0]
    rows = fourier.shape[1] * fourier.shape[2]
    flat = fourier.reshape(lat * rows, fourier.shape[3])
    steps = lat // 8
    out = pl.pallas_call(
        pack_kernel,
        out_shape=pltpu.HBM((24, 2, lat, 128), jnp.float32),
        in_specs=[ANY],
        out_specs=ANY,
        scratch_shapes=[
            pltpu.VMEM((steps, 8 * rows, flat.shape[1]), jnp.float32),
            pltpu.VMEM((steps, 24, 2, 8, 128), jnp.float32),
            pltpu.SemaphoreType.DMA((steps,)),
            pltpu.SemaphoreType.DMA((steps,)),
        ],
        compiler_params=SMALL,
        name="pack",
    )(in_hbm(flat))
    return out.reshape(48, lat, 128)


def edges_kernel(coefs_ref, wet_ref, eta_ref, index_ref, w_low_ref, w_high_ref, fields_ref, places_ref, low_ref, high_ref):
    coefs = coefs_ref[...]
    norm = coefs / jnp.sum(coefs, axis=0)
    fields_ref[0:9] = norm
    fields_ref[9] = wet_ref[...].astype(jnp.float32)
    fields_ref[10] = eta_ref[...]
    first = jnp.transpose(fields_ref[0:8].reshape(128, 128))
    second = jnp.transpose(
        jnp.concatenate(
            [fields_ref[8:11].reshape(48, 128), jnp.zeros((80, 128), jnp.float32)], axis=0
        )
    )
    index = index_ref[...]
    device = (index * 1821) >> 16
    places = ((device & 3) * 12 + (device >> 2)) * PIECE + index - device * 36
    places_ref[...] = places
    for ref, w_ref, at in ((low_ref, w_low_ref, 0), (high_ref, w_high_ref, 120)):
        ref[0:256] = w_ref[...].reshape(256, 128)
        ref[256:264] = first[at : at + 8]
        ref[264:272] = second[at : at + 8]
        ref[272:280] = jnp.zeros((8, 128), jnp.float32)
        ref[272:274, 0:16] = places.astype(jnp.float32)


def edges(coefs, wet, eta, index, weight):
    rows = eta.shape[0]
    message = pltpu.HBM((280, 128), jnp.float32)
    whole = lambda shape: pl.BlockSpec(shape, lambda i: (0,) * len(shape))
    return pl.pallas_call(
        edges_kernel,
        out_shape=(
            jax.ShapeDtypeStruct((FIELDS, rows, 128), jnp.float32),
            jax.ShapeDtypeStruct(index.shape, jnp.int32),
            message,
            message,
        ),
        grid=(1,),
        in_specs=[
            whole(coefs.shape),
            whole(wet.shape),
            whole(eta.shape),
            whole(index.shape),
            pl.BlockSpec((32, 8, 128), lambda i: (0, 0, 0)),
            pl.BlockSpec((32, 8, 128), lambda i: (0, 15, 0)),
        ],
        out_specs=(whole((FIELDS, rows, 128)), whole(index.shape), whole((280, 128)), whole((280, 128))),
        compiler_params=SMALL,
        name="edges",
    )(in_hbm(coefs), in_hbm(wet), in_hbm(eta), in_hbm(index), in_hbm(weight), in_hbm(weight))


def stage(leg_ref, stage_ref, sem):
    part = stage_ref.shape[0] // 2
    copies = [
        pltpu.make_async_copy(
            leg_ref.at[0, pl.ds(i * part, part)],
            stage_ref.at[pl.ds(i * part, part)],
            sem.at[i],
        )
        for i in range(2)
    ]
    for copy in copies:
        copy.start()
    return copies


def forcing_kernel(own_ref, right_ref, left_ref, flux_ref, w_ref, fields_ref, from_right_ref, from_left_ref, top_ref, low_ref, picks):
    for place, ref in enumerate((own_ref, right_ref, left_ref)):
        for i in range(16):
            for k in range(2):
                picks[place, pl.ds(2 * i + k, 1), :] = flux_ref[pl.ds(ref[k, i].astype(jnp.int32), 1), :]
    sub = lax.broadcasted_iota(jnp.int32, (16, 8, 128), 1)
    tile = lax.broadcasted_iota(jnp.int32, (16, 8, 128), 0)
    lane = lax.broadcasted_iota(jnp.int32, (16, 8, 128), 2)
    here = lane == 8 * tile + sub
    for i in range(16):
        acc = w_ref[2 * i] * picks[0, pl.ds(2 * i, 1), :]
        acc = acc + w_ref[2 * i + 1] * picks[0, pl.ds(2 * i + 1, 1), :]
        total = jnp.sum(acc.reshape(16, 8, 128), axis=2, keepdims=True)
        row = jnp.sum(jnp.sum(jnp.where(here, total, 0.0), axis=0), axis=0, keepdims=True)
        ref = top_ref if i < 8 else low_ref
        ref[FIELDS, 0, pl.ds(i % 8, 1), :] = row
    wide_r = (from_right_ref[0:256] * jnp.broadcast_to(picks[1][:, None, :], (32, 8, 128)).reshape(256, 128)).reshape(16, 2, 8, 128)
    wide_l = (from_left_ref[0:256] * jnp.broadcast_to(picks[2][:, None, :], (32, 8, 128)).reshape(256, 128)).reshape(16, 2, 8, 128)
    sum_r = jnp.sum(wide_r[:, 0] + wide_r[:, 1], axis=2, keepdims=True)
    sum_l = jnp.sum(wide_l[:, 0] + wide_l[:, 1], axis=2, keepdims=True)
    outer = jnp.where(lane == sub, sum_r, jnp.where(lane == 120 + sub, sum_l, 0.0))
    outer = jnp.sum(outer, axis=1)
    top_ref[FIELDS, 1] = outer[0:8]
    low_ref[FIELDS, 1] = outer[8:16]
    gap = jnp.zeros((112, 128), jnp.float32)
    side = [
        jnp.transpose(
            jnp.concatenate([from_right_ref[at : at + 8], gap, from_left_ref[at : at + 8]], axis=0)
        ).reshape(8, 16, 128)
        for at in (256, 264)
    ]
    for f in range(FIELDS):
        centre = fields_ref[f]
        beside = side[f // 8][f % 8]
        top_ref[f, 0] = centre[0:8]
        low_ref[f, 0] = centre[8:16]
        top_ref[f, 1] = beside[0:8]
        low_ref[f, 1] = beside[8:16]


def forcing_fields(places, flux, weight, fields, from_right, from_left):
    half = jax.ShapeDtypeStruct((FIELDS + 1, 2, 8, 128), jnp.float32)
    smem = pl.BlockSpec(memory_space=pltpu.SMEM)
    tail = pl.BlockSpec((8, 128), lambda i: (34, 0), memory_space=pltpu.SMEM)
    return pl.pallas_call(
        forcing_kernel,
        out_shape=(half, half),
        grid=(1,),
        in_specs=[smem, tail, tail] + [VMEM] * 5,
        out_specs=(VMEM, VMEM),
        scratch_shapes=[pltpu.VMEM((3, 32, 128), jnp.float32)],
        compiler_params=SMALL,
        name="forcing",
    )(places, from_right, from_left, flux, weight, fields, from_right, from_left)


def relax_kernel(top_ref, low_ref, below_ref, above_ref, leg_ref, out_ref, stage_ref, table, sem):
    copies = stage(leg_ref, stage_ref, sem)
    for f in range(FIELDS + 1):
        for place, ref in enumerate((top_ref, low_ref, below_ref, above_ref)):
            for side in range(2):
                table[f, place * 8 : place * 8 + 8, side * 128 : side * 128 + 128] = ref[f, side]
    norm = []
    for k in range(9):
        value = table[k]
        if k // 3 == 0:
            value = pltpu.roll(value, 31, axis=0)
        if k // 3 == 2:
            value = pltpu.roll(value, 1, axis=0)
        norm.append(value)
    wet = table[9]
    eta = table[10]
    force = FORCING_RATE * table[11]
    for _ in range(SUBS):
        left = pltpu.roll(eta, 1, axis=1)
        right = pltpu.roll(eta, 255, axis=1)
        part = [norm[3 * p] * left + norm[3 * p + 1] * eta + norm[3 * p + 2] * right for p in range(3)]
        total = pltpu.roll(part[0], 1, axis=0) + part[1] + pltpu.roll(part[2], 31, axis=0)
        eta = wet * (total + force)
    out_ref[...] = eta[0:16, 0:128]
    for copy in copies:
        copy.wait()


def relax(top, low, below, above, legendre):
    return pl.pallas_call(
        relax_kernel,
        out_shape=(
            jax.ShapeDtypeStruct((16, 128), jnp.float32),
            pltpu.VMEM((STAGED, legendre.shape[2]), jnp.float32),
        ),
        in_specs=[VMEM] * 4 + [ANY],
        out_specs=(VMEM, VMEM),
        scratch_shapes=[
            pltpu.VMEM((FIELDS + 1, 32, 256), jnp.float32),
            pltpu.SemaphoreType.DMA((2,)),
        ],
        compiler_params=SMALL,
        name="relax",
    )(top, low, below, above, in_hbm(legendre))


def split(value):
    high = value.astype(jnp.bfloat16)
    return high, (value - high.astype(jnp.float32)).astype(jnp.bfloat16)


def contract_kernel(x_ref, staged_ref, leg_ref, spectral_ref, held, done, sem, out_sem):
    parts = held.shape[0]
    depth = held.shape[1]
    staged = STAGED
    reads = [
        pltpu.make_async_copy(source, held.at[i], sem.at[i])
        for i, source in enumerate(
            [leg_ref.at[0, pl.ds(staged, depth)]]
            + [leg_ref.at[1, pl.ds(i * depth, depth)] for i in range(parts - 1)]
        )
    ]
    for read in reads:
        read.start()
    chunks = [held.at[i] for i in range(parts)]
    plan = ([staged_ref, chunks[0]], chunks[1:])
    x_high, x_low = split(jnp.transpose(x_ref[...]))
    dot = lambda a, b: jnp.dot(a, b, preferred_element_type=jnp.float32)
    writes = [
        pltpu.make_async_copy(done.at[m], spectral_ref.at[m], out_sem.at[m]) for m in range(2)
    ]
    waits = iter(reads)
    for m, refs in enumerate(plan):
        mine = slice(m * 64, m * 64 + 64)
        total, start = None, 0
        for i, part_ref in enumerate(refs):
            if m == 1 or i == 1:
                next(waits).wait()
            ends = slice(start, start + part_ref.shape[0])
            start += part_ref.shape[0]
            high, low = split(part_ref[...])
            both = dot(jnp.concatenate([x_high[mine, ends], x_low[mine, ends]], axis=0), high)
            part = both[0:64] + both[64:128] + dot(x_high[mine, ends], low)
            total = part if total is None else total + part
        for r in range(2):
            for v in range(4):
                for l in range(8):
                    row = r * 32 + v * 8 + l
                    done[m, v, l, pl.ds(r, 1), :] = total[row : row + 1]
        writes[m].start()
    for write in writes:
        write.wait()


def contract(x, staged, legendre):
    ms, depth, degrees = legendre.shape
    parts = 4
    return pl.pallas_call(
        contract_kernel,
        out_shape=jax.ShapeDtypeStruct((ms, 4, 8, 2, degrees), jnp.float32),
        in_specs=[VMEM] * 2 + [ANY],
        out_specs=ANY,
        scratch_shapes=[
            pltpu.VMEM((parts, depth // 3, degrees), jnp.float32),
            pltpu.VMEM((ms, 4, 8, 2, degrees), jnp.float32),
            pltpu.SemaphoreType.DMA((parts,)),
            pltpu.SemaphoreType.DMA((ms,)),
        ],
        compiler_params=SMALL,
        name="contract",
    )(x, in_vmem(staged), in_hbm(legendre))


def shifted(value, axis, step):
    count = lax.axis_size(axis)
    pairs = [(i, i + step) for i in range(count) if 0 <= i + step < count]
    return lax.ppermute(value, axis, pairs)


def body(fourier, legendre, eta_start, coefs, wet, src_index, regrid_weight):
    weight = regrid_weight.reshape(32, 128, 128)
    index = jnp.transpose(src_index[:, 0, :])
    pieces = flux_pieces(fourier, 12)
    along = lax.all_to_all(pieces, "dom_0", split_axis=0, concat_axis=0)
    packed = pack(fourier)
    fields, places, low_edge, high_edge = edges(coefs, wet, eta_start, index, weight)
    from_right = shifted(low_edge, DOM, -1)
    from_left = shifted(high_edge, DOM, 1)
    packed, along = lax.optimization_barrier((packed, along))
    block = lax.all_to_all(packed, DOM, split_axis=0, concat_axis=0)
    flux = lax.all_gather(along.reshape(12 * PIECE, 128), "dom_1", axis=0, tiled=True)
    top, low = forcing_fields(places, flux, weight, fields, from_right, from_left)
    below = shifted(top, ROW, -1)
    above = shifted(low, ROW, 1)
    eta, staged = relax(top, low, below, above, legendre)
    spectral = contract(block.reshape(1152, 128), staged, legendre)
    return spectral, eta


def solution(mesh):
    torus = Mesh(
        mesh.devices.reshape(mesh.shape["group"], 12, 4, mesh.shape["sub"]),
        ("group", "dom_0", "dom_1", "sub"),
    )
    in_specs = (
        P(DOM, None, ROW, None),
        P(DOM, None, None),
        P(ROW, DOM),
        P(None, ROW, DOM),
        P(ROW, DOM),
        P(ROW, DOM, None),
        P(ROW, DOM, None, None, None),
    )
    out_specs = (P(DOM, None, ROW, None, None), P(ROW, DOM))

    def step(*args):
        return body(*args)

    step = jax.shard_map(step, mesh=torus, in_specs=in_specs, out_specs=out_specs, check_vma=False)
    return step
```

```python
import jax
import jax.numpy as jnp
from jax import lax
from jax.experimental import pallas as pl
from jax.experimental.pallas import tpu as pltpu
from jax.sharding import Mesh
from jax.sharding import PartitionSpec as P


SUBS = 8
DOM = ("dom_0", "dom_1")
ROW = ("group", "sub")
FORCING_RATE = 0.5
FIELDS = 11
PIECE = 40


VMEM = pl.BlockSpec(memory_space=pltpu.VMEM)
ANY = pl.BlockSpec(memory_space=pl.ANY)
SMALL = pltpu.CompilerParams(vmem_limit_bytes=24 << 20)


def in_vmem(value):
    return pltpu.with_memory_space_constraint(value, pltpu.VMEM)


def in_hbm(value):
    return pltpu.with_memory_space_constraint(value, pltpu.HBM)


def flux_kernel(fourier_ref, out_ref, surface, sem):
    copy = pltpu.make_async_copy(fourier_ref.at[:, 0, pl.ds(0, 1), :], surface, sem)
    copy.start()
    copy.wait()
    rows = []
    for pair in range(surface.shape[0] // 2):
        a = surface[2 * pair]
        b = surface[2 * pair + 1]
        rows.append(a[:, :128])
        rows.append(jnp.concatenate([a[:, 128:], b[:, :64]], axis=1))
        rows.append(b[:, 64:])
    rows.append(jnp.zeros((PIECE - len(rows), 128), jnp.float32))
    piece = jnp.concatenate(rows, axis=0)
    for i in range(out_ref.shape[0]):
        out_ref[i] = piece


def flux_pieces(fourier, copies):
    lat, cols = fourier.shape[0], fourier.shape[3]
    return pl.pallas_call(
        flux_kernel,
        out_shape=pltpu.VMEM((copies, PIECE, 128), jnp.float32),
        in_specs=[ANY],
        out_specs=VMEM,
        scratch_shapes=[pltpu.VMEM((lat, 1, cols), jnp.float32), pltpu.SemaphoreType.DMA(())],
        compiler_params=SMALL,
        name="flux_pieces",
    )(in_hbm(fourier))


def pack_kernel(all_ref, packed_ref, inside, outside, in_sem, out_sem):
    chunk = inside.shape[1]
    steps = inside.shape[0]
    reads = [
        pltpu.make_async_copy(all_ref.at[pl.ds(i * chunk, chunk)], inside.at[i], in_sem.at[i])
        for i in range(steps)
    ]
    writes = [
        pltpu.make_async_copy(outside.at[i], packed_ref.at[:, :, pl.ds(8 * i, 8)], out_sem.at[i])
        for i in range(steps)
    ]
    for read in reads:
        read.start()
    for read, write, x_ref, out_ref in zip(reads, writes, map(inside.at.__getitem__, range(steps)), map(outside.at.__getitem__, range(steps))):
        read.wait()
        pack_latitudes(x_ref, out_ref)
        write.start()
    for write in writes:
        write.wait()


def pack_latitudes(x_ref, out_ref):
    turn = lax.broadcasted_iota(jnp.int32, (32, 128), 1) % 4
    tiles = []
    for part in range(3):
        lats = []
        for j in range(4):
            if part < 2:
                lats.append(x_ref[pl.ds((4 * part + j) * 32, 32), 0:128])
            else:
                ends = [x_ref[pl.ds((4 * half + j) * 32, 32), 128:192] for half in range(2)]
                lats.append(jnp.concatenate(ends, axis=1))
        groups = []
        for c in range(4):
            moved = [x if j == c else pltpu.roll(x, (j - c) % 128, axis=1) for j, x in enumerate(lats)]
            low = jnp.where(turn == 0, moved[0], moved[1])
            high = jnp.where(turn == 2, moved[2], moved[3])
            groups.append(jnp.where(turn < 2, low, high))
        tiles.append(jnp.transpose(jnp.concatenate(groups, axis=0)))
    first = jnp.concatenate([tiles[0], tiles[2][0:64]], axis=0).reshape(24, 8, 128)
    second = jnp.concatenate([tiles[1], tiles[2][64:128]], axis=0).reshape(24, 8, 128)
    upper = lax.broadcasted_iota(jnp.int32, (24, 8, 128), 1) < 4
    out_ref[:, 0] = jnp.where(upper, first, pltpu.roll(second, 4, axis=1))
    out_ref[:, 1] = jnp.where(upper, pltpu.roll(first, 4, axis=1), second)


def pack(fourier):
    lat = fourier.shape[0]
    rows = fourier.shape[1] * fourier.shape[2]
    flat = fourier.reshape(lat * rows, fourier.shape[3])
    steps = lat // 8
    out = pl.pallas_call(
        pack_kernel,
        out_shape=pltpu.HBM((24, 2, lat, 128), jnp.float32),
        in_specs=[ANY],
        out_specs=ANY,
        scratch_shapes=[
            pltpu.VMEM((steps, 8 * rows, flat.shape[1]), jnp.float32),
            pltpu.VMEM((steps, 24, 2, 8, 128), jnp.float32),
            pltpu.SemaphoreType.DMA((steps,)),
            pltpu.SemaphoreType.DMA((steps,)),
        ],
        compiler_params=SMALL,
        name="pack",
    )(in_hbm(flat))
    return out.reshape(48, lat, 128)


def edges_kernel(coefs_ref, wet_ref, eta_ref, index_ref, w_low_ref, w_high_ref, fields_ref, places_ref, low_ref, high_ref):
    coefs = coefs_ref[...]
    norm = coefs / jnp.sum(coefs, axis=0)
    fields_ref[0:9] = norm
    fields_ref[9] = wet_ref[...].astype(jnp.float32)
    fields_ref[10] = eta_ref[...]
    first = jnp.transpose(fields_ref[0:8].reshape(128, 128))
    second = jnp.transpose(
        jnp.concatenate(
            [fields_ref[8:11].reshape(48, 128), jnp.zeros((80, 128), jnp.float32)], axis=0
        )
    )
    index = index_ref[...]
    device = (index * 1821) >> 16
    places = ((device & 3) * 12 + (device >> 2)) * PIECE + index - device * 36
    places_ref[...] = places
    for ref, w_ref, at in ((low_ref, w_low_ref, 0), (high_ref, w_high_ref, 120)):
        ref[0:256] = w_ref[...].reshape(256, 128)
        ref[256:264] = first[at : at + 8]
        ref[264:272] = second[at : at + 8]
        ref[272:280] = jnp.zeros((8, 128), jnp.float32)
        ref[272:274, 0:16] = places.astype(jnp.float32)


def edges(coefs, wet, eta, index, weight):
    rows = eta.shape[0]
    message = pltpu.HBM((280, 128), jnp.float32)
    whole = lambda shape: pl.BlockSpec(shape, lambda i: (0,) * len(shape))
    return pl.pallas_call(
        edges_kernel,
        out_shape=(
            jax.ShapeDtypeStruct((FIELDS, rows, 128), jnp.float32),
            jax.ShapeDtypeStruct(index.shape, jnp.int32),
            message,
            message,
        ),
        grid=(1,),
        in_specs=[
            whole(coefs.shape),
            whole(wet.shape),
            whole(eta.shape),
            whole(index.shape),
            pl.BlockSpec((32, 8, 128), lambda i: (0, 0, 0)),
            pl.BlockSpec((32, 8, 128), lambda i: (0, 15, 0)),
        ],
        out_specs=(whole((FIELDS, rows, 128)), whole(index.shape), whole((280, 128)), whole((280, 128))),
        compiler_params=SMALL,
        name="edges",
    )(in_hbm(coefs), in_hbm(wet), in_hbm(eta), in_hbm(index), in_hbm(weight), in_hbm(weight))


def stage(leg_ref, stage_ref, sem):
    part = stage_ref.shape[0] // 2
    copies = [
        pltpu.make_async_copy(
            leg_ref.at[0, pl.ds(i * part, part)],
            stage_ref.at[pl.ds(i * part, part)],
            sem.at[i],
        )
        for i in range(2)
    ]
    for copy in copies:
        copy.start()
    return copies


def forcing_kernel(own_ref, right_ref, left_ref, flux_ref, w_ref, fields_ref, from_right_ref, from_left_ref, top_ref, low_ref, picks):
    for place, ref in enumerate((own_ref, right_ref, left_ref)):
        for i in range(16):
            for k in range(2):
                picks[place, pl.ds(2 * i + k, 1), :] = flux_ref[pl.ds(ref[k, i].astype(jnp.int32), 1), :]
    sub = lax.broadcasted_iota(jnp.int32, (16, 8, 128), 1)
    tile = lax.broadcasted_iota(jnp.int32, (16, 8, 128), 0)
    lane = lax.broadcasted_iota(jnp.int32, (16, 8, 128), 2)
    here = lane == 8 * tile + sub
    for i in range(16):
        acc = w_ref[2 * i] * picks[0, pl.ds(2 * i, 1), :]
        acc = acc + w_ref[2 * i + 1] * picks[0, pl.ds(2 * i + 1, 1), :]
        total = jnp.sum(acc.reshape(16, 8, 128), axis=2, keepdims=True)
        row = jnp.sum(jnp.sum(jnp.where(here, total, 0.0), axis=0), axis=0, keepdims=True)
        ref = top_ref if i < 8 else low_ref
        ref[FIELDS, 0, pl.ds(i % 8, 1), :] = row
    wide_r = (from_right_ref[0:256] * jnp.broadcast_to(picks[1][:, None, :], (32, 8, 128)).reshape(256, 128)).reshape(16, 2, 8, 128)
    wide_l = (from_left_ref[0:256] * jnp.broadcast_to(picks[2][:, None, :], (32, 8, 128)).reshape(256, 128)).reshape(16, 2, 8, 128)
    sum_r = jnp.sum(wide_r[:, 0] + wide_r[:, 1], axis=2, keepdims=True)
    sum_l = jnp.sum(wide_l[:, 0] + wide_l[:, 1], axis=2, keepdims=True)
    outer = jnp.where(lane == sub, sum_r, jnp.where(lane == 120 + sub, sum_l, 0.0))
    outer = jnp.sum(outer, axis=1)
    top_ref[FIELDS, 1] = outer[0:8]
    low_ref[FIELDS, 1] = outer[8:16]
    gap = jnp.zeros((112, 128), jnp.float32)
    side = [
        jnp.transpose(
            jnp.concatenate([from_right_ref[at : at + 8], gap, from_left_ref[at : at + 8]], axis=0)
        ).reshape(8, 16, 128)
        for at in (256, 264)
    ]
    for f in range(FIELDS):
        centre = fields_ref[f]
        beside = side[f // 8][f % 8]
        top_ref[f, 0] = centre[0:8]
        low_ref[f, 0] = centre[8:16]
        top_ref[f, 1] = beside[0:8]
        low_ref[f, 1] = beside[8:16]


def forcing_fields(places, flux, weight, fields, from_right, from_left):
    half = jax.ShapeDtypeStruct((FIELDS + 1, 2, 8, 128), jnp.float32)
    smem = pl.BlockSpec(memory_space=pltpu.SMEM)
    tail = pl.BlockSpec((8, 128), lambda i: (34, 0), memory_space=pltpu.SMEM)
    return pl.pallas_call(
        forcing_kernel,
        out_shape=(half, half),
        grid=(1,),
        in_specs=[smem, tail, tail] + [VMEM] * 5,
        out_specs=(VMEM, VMEM),
        scratch_shapes=[pltpu.VMEM((3, 32, 128), jnp.float32)],
        compiler_params=SMALL,
        name="forcing",
    )(places, from_right, from_left, flux, weight, fields, from_right, from_left)


def relax_kernel(top_ref, low_ref, below_ref, above_ref, leg_ref, out_ref, stage_ref, table, sem):
    copies = stage(leg_ref, stage_ref, sem)
    for f in range(FIELDS + 1):
        for place, ref in enumerate((top_ref, low_ref, below_ref, above_ref)):
            for side in range(2):
                table[f, place * 8 : place * 8 + 8, side * 128 : side * 128 + 128] = ref[f, side]
    norm = []
    for k in range(9):
        value = table[k]
        if k // 3 == 0:
            value = pltpu.roll(value, 31, axis=0)
        if k // 3 == 2:
            value = pltpu.roll(value, 1, axis=0)
        norm.append(value)
    wet = table[9]
    eta = table[10]
    force = FORCING_RATE * table[11]
    for _ in range(SUBS):
        left = pltpu.roll(eta, 1, axis=1)
        right = pltpu.roll(eta, 255, axis=1)
        part = [norm[3 * p] * left + norm[3 * p + 1] * eta + norm[3 * p + 2] * right for p in range(3)]
        total = pltpu.roll(part[0], 1, axis=0) + part[1] + pltpu.roll(part[2], 31, axis=0)
        eta = wet * (total + force)
    out_ref[...] = eta[0:16, 0:128]
    for copy in copies:
        copy.wait()


def relax(top, low, below, above, legendre):
    return pl.pallas_call(
        relax_kernel,
        out_shape=(
            jax.ShapeDtypeStruct((16, 128), jnp.float32),
            pltpu.VMEM(legendre.shape[1:], jnp.float32),
        ),
        in_specs=[VMEM] * 4 + [ANY],
        out_specs=(VMEM, VMEM),
        scratch_shapes=[
            pltpu.VMEM((FIELDS + 1, 32, 256), jnp.float32),
            pltpu.SemaphoreType.DMA((2,)),
        ],
        compiler_params=SMALL,
        name="relax",
    )(top, low, below, above, in_hbm(legendre))


def split(value):
    high = value.astype(jnp.bfloat16)
    return high, (value - high.astype(jnp.float32)).astype(jnp.bfloat16)


def contract_kernel(x_ref, staged_ref, leg_ref, spectral_ref, held, done, sem, out_sem):
    reads, chunks, start = [], [], 0
    for i, length in enumerate((512, 384, 256)):
        part = held.at[pl.ds(start, length)]
        reads.append(
            pltpu.make_async_copy(leg_ref.at[1, pl.ds(start, length)], part, sem.at[i])
        )
        chunks.append(part)
        start += length
    for read in reads:
        read.start()
    x_high, x_low = split(jnp.transpose(x_ref[...]))
    dot = lambda a, b: jnp.dot(a, b, preferred_element_type=jnp.float32)
    writes = [
        pltpu.make_async_copy(done.at[m], spectral_ref.at[m], out_sem.at[m]) for m in range(2)
    ]
    for m, refs in enumerate(([staged_ref], chunks)):
        mine = slice(m * 64, m * 64 + 64)
        total, start = None, 0
        for i, part_ref in enumerate(refs):
            if m == 1:
                reads[i].wait()
            ends = slice(start, start + part_ref.shape[0])
            start += part_ref.shape[0]
            high, low = split(part_ref[...])
            both = dot(jnp.concatenate([x_high[mine, ends], x_low[mine, ends]], axis=0), high)
            part = both[0:64] + both[64:128] + dot(x_high[mine, ends], low)
            total = part if total is None else total + part
        for r in range(2):
            for v in range(4):
                for l in range(8):
                    row = r * 32 + v * 8 + l
                    done[m, v, l, pl.ds(r, 1), :] = total[row : row + 1]
        writes[m].start()
    for write in writes:
        write.wait()


def contract(x, staged, legendre):
    ms, depth, degrees = legendre.shape
    return pl.pallas_call(
        contract_kernel,
        out_shape=jax.ShapeDtypeStruct((ms, 4, 8, 2, degrees), jnp.float32),
        in_specs=[VMEM] * 2 + [ANY],
        out_specs=ANY,
        scratch_shapes=[
            pltpu.VMEM((depth, degrees), jnp.float32),
            pltpu.VMEM((ms, 4, 8, 2, degrees), jnp.float32),
            pltpu.SemaphoreType.DMA((3,)),
            pltpu.SemaphoreType.DMA((ms,)),
        ],
        compiler_params=SMALL,
        name="contract",
    )(x, in_vmem(staged), in_hbm(legendre))


def shifted(value, axis, step):
    count = lax.axis_size(axis)
    pairs = [(i, i + step) for i in range(count) if 0 <= i + step < count]
    return lax.ppermute(value, axis, pairs)


def body(fourier, legendre, eta_start, coefs, wet, src_index, regrid_weight):
    weight = regrid_weight.reshape(32, 128, 128)
    index = jnp.transpose(src_index[:, 0, :])
    pieces = flux_pieces(fourier, 12)
    along = lax.all_to_all(pieces, "dom_0", split_axis=0, concat_axis=0)
    packed, coefs = lax.optimization_barrier((pack(fourier), coefs))
    fields, places, low_edge, high_edge = edges(coefs, wet, eta_start, index, weight)
    from_right = shifted(low_edge, DOM, -1)
    from_left = shifted(high_edge, DOM, 1)
    packed, along = lax.optimization_barrier((packed, along))
    block = lax.all_to_all(packed, DOM, split_axis=0, concat_axis=0)
    flux = lax.all_gather(along.reshape(12 * PIECE, 128), "dom_1", axis=0, tiled=True)
    top, low = forcing_fields(places, flux, weight, fields, from_right, from_left)
    below = shifted(top, ROW, -1)
    above = shifted(low, ROW, 1)
    eta, staged = relax(top, low, below, above, legendre)
    spectral = contract(block.reshape(1152, 128), staged, legendre)
    return spectral, eta


def solution(mesh):
    torus = Mesh(
        mesh.devices.reshape(mesh.shape["group"], 12, 4, mesh.shape["sub"]),
        ("group", "dom_0", "dom_1", "sub"),
    )
    in_specs = (
        P(DOM, None, ROW, None),
        P(DOM, None, None),
        P(ROW, DOM),
        P(None, ROW, DOM),
        P(ROW, DOM),
        P(ROW, DOM, None),
        P(ROW, DOM, None, None, None),
    )
    out_specs = (P(DOM, None, ROW, None, None), P(ROW, DOM))

    def step(*args):
        return body(*args)

    step = jax.shard_map(step, mesh=torus, in_specs=in_specs, out_specs=out_specs, check_vma=False)
    return step
```
